128 devices in a mesh: row: 16 (over y, x), col: 8 (over z, core).
Axes of the slice: x: 4, y: 4, z: 4, core: 2. Of those that a mesh axis runs over, the one named last changes fastest.
Arguments:
- gain_pair: float32 [2], replicated, may hold values from 0.5 to 2
- weight_up: bfloat16 [24576, 6144], P('row', 'col'), as said below
- weight_down: bfloat16 [6144, 24576], P('row', 'col'), as said below
- inputs_up: bfloat16 [3072, 6144], P('row', 'col'), may hold values from -8 to 8, as said below
- grads_up: bfloat16 [3072, 24576], P('col', 'row'), may hold values from -0.125 to 0.125, as said below
- inputs_down: bfloat16 [3072, 24576], P('row', 'col'), may hold values from -8 to 8, as said below
- grads_down: bfloat16 [3072, 6144], P('col', 'row'), may hold values from -0.125 to 0.125, as said below
- vector_up: float32 [6144], P('col'), may hold values from -6 to 6
- vector_down: float32 [24576], P('col'), may hold values from -6 to 6
Outputs:
- wgrad_up: bfloat16 [24576, 6144], P('row', 'col')
- wgrad_down: bfloat16 [6144, 24576], P('row', 'col')
- gain_grads: float32 [2], replicated
- left_up: float32 [24576], P('row')
- right_up: float32 [6144], P('col')
- left_down: float32 [6144], P('row')
- right_down: float32 [24576], P('col')
The draws below stay inside these ranges and needn't reach their ends.
Inputs may be any that keep to these rules, and one draw needn't show every extreme that they name: `weight_up`: drawn afresh from the seed for every entry. `weight_down`: drawn afresh from the seed for every entry. `inputs_up`: drawn afresh from the seed for every entry. `inputs_down`: drawn afresh from the seed for every entry. `grads_up`: drawn afresh from the seed for every entry. `grads_down`: drawn afresh from the seed for every entry.
All inputs are finite; a program needn't handle non-finite values.
Results may differ from the reference program's by a relative error of at most 0.007.
Values may be sent and summed in bfloat16 or wider, within the bound.
A program may use at most 128 MiB of HBM per device.

```python
import jax
import jax.numpy as jnp
from jax import lax

D = 6144
FF = 24576
ITERS = 2
TOKENS = 3072


def shared(key, tag, count, factor):
    base = jax.random.normal(jax.random.fold_in(key, tag), (count,), jnp.float32)
    return jnp.clip(base, -4.0, 4.0) * factor


def noise(key, tag, shape, limit):
    return jnp.clip(jax.random.normal(jax.random.fold_in(key, tag), shape, jnp.float32), -limit, limit)


def draw_weight_up(key, part):
    rows_q = shared(key, 11, FF, 0.1)
    cols_p = shared(key, 12, D, 0.1)
    return (noise(key, 103, (FF, D), 6.0) * D ** (-0.5) + 0.05 * rows_q[:, None] * cols_p[None, :]).astype(jnp.bfloat16)


def draw_inputs_up(key, part):
    tokens_a = shared(key, 13, TOKENS, 1.0)
    cols_p = shared(key, 12, D, 0.1)
    return jnp.clip(noise(key, 101, (TOKENS, D), 6.0) + tokens_a[:, None] * cols_p[None, :], -8.0, 8.0).astype(jnp.bfloat16)


def draw_grads_up(key, part):
    tokens_a = shared(key, 13, TOKENS, 1.0)
    rows_q = shared(key, 11, FF, 0.1)
    return (jnp.clip(noise(key, 102, (TOKENS, FF), 6.0) + tokens_a[:, None] * rows_q[None, :], -8.0, 8.0) / 64.0).astype(jnp.bfloat16)


def draw_weight_down(key, part):
    rows_q = shared(key, 21, D, 0.1)
    cols_p = shared(key, 22, FF, 0.1)
    return (noise(key, 203, (D, FF), 6.0) * FF ** (-0.5) + 0.05 * rows_q[:, None] * cols_p[None, :]).astype(jnp.bfloat16)


def draw_inputs_down(key, part):
    tokens_a = shared(key, 23, TOKENS, 1.0)
    cols_p = shared(key, 22, FF, 0.1)
    return jnp.clip(noise(key, 201, (TOKENS, FF), 6.0) + tokens_a[:, None] * cols_p[None, :], -8.0, 8.0).astype(jnp.bfloat16)


def draw_grads_down(key, part):
    tokens_a = shared(key, 23, TOKENS, 1.0)
    rows_q = shared(key, 21, D, 0.1)
    return (jnp.clip(noise(key, 202, (TOKENS, D), 6.0) + tokens_a[:, None] * rows_q[None, :], -8.0, 8.0) / 64.0).astype(jnp.bfloat16)


def block_scale(key, extent, split, smallest, top_value):
    level = 1.0
    for position, parts in split:
        draws = jax.random.uniform(jax.random.fold_in(jax.random.fold_in(key, 6), position), (parts,), jnp.float32, smallest / len(split), top_value / len(split))
        level = level * jnp.repeat(jnp.exp(draws), extent[position] // parts).reshape((-1,) + (1,) * (len(extent) - 1 - position))
    return level


def normal_values(own_key, dims, scale, most, shards=(), held_as=jnp.bfloat16):
    factor_of = block_scale(own_key, dims, shards, -0.22, 0.18) if shards else 1.0
    array = jax.random.normal(own_key, dims, jnp.float32) * scale * factor_of
    return jnp.minimum(jnp.maximum(array, -most), most).astype(held_as)


def setup_inputs(seed: int = 0) -> dict:
    key_list = jax.random.split(jax.random.key(seed), 10)
    gain_pair = jnp.clip(jax.random.uniform(key_list[0], (2,), jnp.float32, 0.5, 2.0), 0.5, 2.0)
    weight_up = draw_weight_up(jax.random.fold_in(key_list[9], 71), 0)
    weight_down = draw_weight_down(jax.random.fold_in(key_list[9], 71), 0)
    inputs_up = draw_inputs_up(jax.random.fold_in(key_list[9], 71), 0)
    grads_up = draw_grads_up(jax.random.fold_in(key_list[9], 71), 0)
    inputs_down = draw_inputs_down(jax.random.fold_in(key_list[9], 71), 0)
    grads_down = draw_grads_down(jax.random.fold_in(key_list[9], 71), 0)
    vector_up = normal_values(key_list[7], (D,), 1.0, 6.0, ((0, 8),), jnp.float32)
    vector_down = normal_values(key_list[8], (FF,), 1.0, 6.0, ((0, 8),), jnp.float32)
    return {"gain_pair": gain_pair, "weight_up": weight_up, "weight_down": weight_down, "inputs_up": inputs_up, "grads_up": grads_up, "inputs_down": inputs_down, "grads_down": grads_down, "vector_up": vector_up, "vector_down": vector_down}


def project(weight, inputs, grads, vector, gain):
    grad_w = lax.dot_general(grads, inputs, (((0,), (0,)), ((), ())), preferred_element_type=jnp.float32)
    right = vector
    left = vector
    left_b = vector.astype(jnp.bfloat16)
    sigma = jnp.float32(1.0)
    for step in range(ITERS):
        right_b = right.astype(jnp.bfloat16)
        prod_s = jnp.dot(weight, right_b, preferred_element_type=jnp.float32)
        left = prod_s / jnp.sqrt(jnp.sum(prod_s * prod_s) + 1e-06)
        left_b = left.astype(jnp.bfloat16)
        prod_t = jnp.dot(left_b, weight, preferred_element_type=jnp.float32)
        if step + 1 < ITERS:
            right = prod_t
        else:
            sigma = jnp.sqrt(jnp.sum(prod_t * prod_t) + 1e-06)
            right = prod_t / sigma
    inner = jnp.sum(grad_w * weight.astype(jnp.float32))
    outer = left_b.astype(jnp.float32)[:, None] * right[None, :]
    wgrad = (gain / sigma * grad_w - gain * inner / (sigma * sigma) * outer).astype(jnp.bfloat16)
    return (wgrad, inner / sigma, left, right)

def reference(gain_pair, weight_up, weight_down, inputs_up, grads_up, inputs_down, grads_down, vector_up, vector_down):
    wgrad_up, gain_a, left_up, right_up = project(weight_up, inputs_up, grads_up, vector_up, gain_pair[0])
    wgrad_down, gain_b, left_down, right_down = project(weight_down, inputs_down, grads_down, vector_down, gain_pair[1])
    gain_grads = jnp.stack([gain_a, gain_b]).astype(jnp.float32)
    return (wgrad_up, wgrad_down, gain_grads, left_up, right_up, left_down, right_down)
```

```python
import jax
import jax.numpy as jnp
from jax import lax
from jax.experimental import pallas as pl
from jax.experimental.pallas import tpu as pltpu
from jax.sharding import PartitionSpec as P

ITERS = 2
MESH = pl.DeviceIdType.MESH
F32 = jnp.float32
BF16 = jnp.bfloat16

TOK = 192
MU, MD = 1536, 384
NU, ND = 768, 3072
T = 3072
TC = 384
NALL = NU + ND
MALL = MU + MD
Q = ND // 4


def shift(i, d, n):
    return lax.rem(i + (d + n), n)


def lanes(v):
    total = v[:, 0:128]
    for k in range(128, v.shape[1], 128):
        total = total + v[:, k : k + 128]
    return total


def kernel(
    gain, wu_h, wd_h, xu_h, yu_h, xd_h, yd_h, vu_in, vd_in,
    ou, od, gg, lu, ru, ld, rd,
    xu, xd, yt, ystage, wu, wd, gu, gsend, gdown, relay, gwacc, ucol,
    e_core, e_z, e_x, e_y, f_core, f_z, f_x, f_y,
    load_sem, store_sem, as_, ar, xs, xr, ys, yr, zs, zr, os_, or_, es, er, fs, fr,
):
    row = lax.axis_index("row")
    col = lax.axis_index("col")
    y, x = lax.div(row, 4), lax.rem(row, 4)
    z, core = lax.div(col, 2), lax.rem(col, 2)

    def at_x(i):
        return {"row": y * 4 + i, "col": col}

    def at_y(i):
        return {"row": i * 4 + x, "col": col}

    def at_z(i):
        return {"row": row, "col": i * 2 + core}

    def at_core(i):
        return {"row": row, "col": z * 2 + i}

    barrier = pltpu.get_barrier_semaphore()
    for d in (1, 2, 3):
        pl.semaphore_signal(barrier, inc=1, device_id=at_x(shift(x, d, 4)), device_id_type=MESH)
        pl.semaphore_signal(barrier, inc=1, device_id=at_y(shift(y, d, 4)), device_id_type=MESH)
        pl.semaphore_signal(barrier, inc=1, device_id=at_z(shift(z, d, 4)), device_id_type=MESH)
    pl.semaphore_signal(barrier, inc=1, device_id=at_core(1 - core), device_id_type=MESH)

    def half_rows(start, size, part):
        return pl.ds(start, size) if part is None else pl.ds(start + part * (size // 2), size // 2)

    def own_half(part):
        return pl.ds(0, TOK) if part is None else pl.ds(part * (TOK // 2), TOK // 2)

    def slots(part):
        return pl.ds(0, 4) if part is None else pl.ds(part * 2, 2)

    def tokens_of(i):
        return pl.ds(pl.multiple_of((i * 2 + core) * TC, 128), TC)

    loads = [
        pltpu.make_async_copy(wu_h, wu, load_sem.at[0]),
        pltpu.make_async_copy(wd_h, wd, load_sem.at[1]),
        pltpu.make_async_copy(xd_h.at[:, pl.ds(pl.multiple_of(x * Q, 128), Q)], xd.at[y, x], load_sem.at[2]),
        pltpu.make_async_copy(xu_h, xu.at[y, x], load_sem.at[3]),
        pltpu.make_async_copy(yd_h, ystage.at[:, pl.ds(MU, MD)], load_sem.at[4]),
        pltpu.make_async_copy(yu_h, ystage.at[:, pl.ds(0, MU)], load_sem.at[5]),
    ]
    for c in (4, 2, 5, 0, 1, 3):
        loads[c].start()

    sent = []

    def remote(ref, dst_ref, send, recv, device):
        return pltpu.make_async_remote_copy(
            src_ref=ref, dst_ref=dst_ref, send_sem=send, recv_sem=recv,
            device_id=device, device_id_type=MESH,
        )

    def go(copies):
        for c in copies:
            c.start()
            sent.append(c)

    def arrived(copies):
        for c in copies:
            c.wait_recv()

    class Ring:
        def __init__(self, me, where, region, send, recv, other=None):
            up, down = where(shift(me, 1, 4)), where(shift(me, -1, 4))

            def copy(o, part, device, k):
                ref = region(o, part)
                return remote(ref, ref, send.at[k], recv.at[k], device)

            self.a = lambda: [copy(0, None, up, 0), copy(0, None, down, 1)]
            self.b = lambda: [copy(-1, 0, up, 2), copy(1, 1, down, 3)]
            self.to_other = lambda k: copy((0, -1, 1, 2)[k], None, other, 4 + k)
            self.other = other is not None

        def full(self):
            go(self.a())
            if self.other:
                go([self.to_other(0)])

        def half(self):
            arrived(self.a())
            go(self.b())
            if self.other:
                go([self.to_other(1), self.to_other(2)])

        def done(self):
            arrived(self.b())
            if self.other:
                go([self.to_other(3)])

        def fin(self):
            arrived([self.to_other(k) for k in range(4)])

    def quarter(d):
        q = shift(x, d, 4)
        return remote(
            xd_h.at[:, pl.ds(pl.multiple_of(q * Q, 128), Q)], xd.at[y, x], as_.at[d - 1], ar.at[d - 1], at_x(q)
        )

    offs = (0, -1, 1, 2)
    xd_y = [
        Ring(y, at_y, lambda o, part, s=s: xd.at[shift(y, o, 4), shift(x, s, 4), own_half(part)], ys.at[k], yr.at[k])
        for k, s in enumerate(offs)
    ]
    xu_x = Ring(x, at_x, lambda o, part: xu.at[y, shift(x, o, 4), own_half(part)], xs.at[0], xr.at[0])
    xu_y = [
        Ring(
            y, at_y, lambda o, part, j=j: xu.at[shift(y, o, 4), slots(part), :, pl.ds(j * 256, 256)],
            ys.at[4 + j], yr.at[4 + j],
        )
        for j in range(3)
    ]

    yd_x = Ring(
        x, at_x,
        lambda o, part: yt.at[0, half_rows(shift(x, o, 4) * MD, MD, part), tokens_of(z)],
        xs.at[1], xr.at[1],
    )
    other = at_core(1 - core)
    yd_z = [
        Ring(
            z, at_z,
            lambda o, part, s=s: yt.at[0, half_rows(shift(x, s, 4) * MD, MD, part), tokens_of(shift(z, o, 4))],
            zs.at[k], zr.at[k], other,
        )
        for k, s in enumerate(offs)
    ]
    yu_z = [
        Ring(
            z, at_z, lambda o, part, j=j: yt.at[1, half_rows(j * 512, 512, part), tokens_of(shift(z, o, 4))],
            zs.at[4 + j], zr.at[4 + j], other,
        )
        for j in range(3)
    ]

    def xchg(buf, n, me, where, send, recv):
        return [
            remote(buf.at[me], buf.at[me], send.at[d - 1], recv.at[d - 1], where(shift(me, d, n)))
            for d in range(1, n)
        ]

    def put(buf, n, me, where, send, recv, value):
        buf[me] = value
        copies = xchg(buf, n, me, where, send, recv)
        for c in copies:
            c.start()
            sent.append(c)
        return copies

    def get(buf, n, copies):
        for c in copies:
            c.wait_recv()
        total = buf[0]
        for k in range(1, n):
            total = total + buf[k]
        return total

    def rows16(v):
        return jnp.broadcast_to(v, (16, v.shape[1])).astype(BF16)

    state = {"vu": None, "vd": None}

    def s_send(it):
        if it == 0:
            vu, vd = vu_in[...], vd_in[...]
        else:
            vu, vd = t_fin(it - 1)
        nt = (((1,), (1,)), ((), ()))
        su = lax.dot_general(rows16(vu), wu[...], nt, preferred_element_type=F32)[0:1]
        sd = lax.dot_general(rows16(vd), wd[...], nt, preferred_element_type=F32)[0:1]
        state["c"] = put(
            e_core.at[it], 2, core, at_core, es.at[it, 0], er.at[it, 0],
            jnp.concatenate([su, sd], axis=1),
        )

    def s_z(it):
        v = get(e_core.at[it], 2, state["c"])
        state["c"] = put(e_z.at[it], 4, z, at_z, es.at[it, 1], er.at[it, 1], v)

    def t_x(it):
        s = get(e_z.at[it], 4, state["c"])
        su, sd = s[:, :MU], s[:, MU:]
        state["s"] = (su, sd)
        tu = jnp.dot(rows16(su), wu[...], preferred_element_type=F32)[0:1]
        td = jnp.dot(rows16(sd), wd[...], preferred_element_type=F32)[0:1]
        v = jnp.concatenate([tu, td, lanes(su * su), lanes(sd * sd)], axis=1)
        state["c"] = put(e_x.at[it], 4, x, at_x, es.at[it, 2], er.at[it, 2], v)

    def t_y(it):
        v = get(e_x.at[it], 4, state["c"])
        state["c"] = put(e_y.at[it], 4, y, at_y, es.at[it, 3], er.at[it, 3], v)

    def t_fin(it):
        v = get(e_y.at[it], 4, state["c"])
        nu = jnp.sqrt(jnp.sum(v[:, NALL : NALL + 128], axis=1, keepdims=True) + 1e-06)
        nd = jnp.sqrt(jnp.sum(v[:, NALL + 128 :], axis=1, keepdims=True) + 1e-06)
        tu, td = v[:, :NU] / nu, v[:, NU:NALL] / nd
        if it + 1 == ITERS:
            su, sd = state["s"]
            uu, ud = su / nu, sd / nd
            lu[...] = uu
            ld[...] = ud
            ru[...] = tu
            rd[...] = td
            ub = jnp.concatenate([uu, ud], axis=1).astype(BF16).astype(F32)
            for s in range(0, MALL, 128):
                ucol[s : s + 128, :] = jnp.broadcast_to(ub[:, s : s + 128], (128, 128)).T
        return tu, td

    def product(which, xref, m0, tm, n0):
        xs_ = xref[:, :, :, pl.ds(pl.multiple_of(n0, 128), 256)].reshape(T, 256)
        return jnp.dot(yt[which, pl.ds(pl.multiple_of(m0, 128), tm), :], xs_, preferred_element_type=F32)

    def up(m, n):
        @pl.loop(0, 2)
        def _(k):
            rows, cols = pl.ds(pl.multiple_of(m * 512 + k * 256, 128), 256), pl.ds(n * 256, 256)
            g = product(1, xu, m * 512 + k * 256, 256, n * 256)
            gu[rows, cols] = g
            prod = g * wu[rows, cols].astype(F32)
            gwacc[0] += jnp.sum(prod.reshape(32, 8, 256), axis=0)

    def out_copies(o):
        if o == 2:
            return [
                remote(gsend.at[0, pl.ds(0, 192)], relay.at[0], os_.at[0], or_.at[0], at_x(shift(x, 1, 4))),
                remote(gsend.at[0, pl.ds(192, 192)], relay.at[1], os_.at[1], or_.at[1], at_x(shift(x, -1, 4))),
            ]
        k = 2 if o == 1 else 3
        return [remote(gsend.at[k - 1], gdown.at[x], os_.at[k], or_.at[k], at_x(shift(x, o, 4)))]

    def relays():
        return [
            remote(relay.at[0], gdown.at[shift(x, -1, 4), pl.ds(0, 192)], os_.at[4], or_.at[4], at_x(shift(x, 1, 4))),
            remote(relay.at[1], gdown.at[shift(x, 1, 4), pl.ds(192, 192)], os_.at[5], or_.at[5], at_x(shift(x, -1, 4))),
        ]

    def down(o):
        dst = gdown.at[x] if o == 0 else gsend.at[{2: 0, 1: 1, -1: 2}[o]]

        @pl.loop(0, Q // 256)
        def _(k):
            g = product(0, xd, shift(x, o, 4) * MD, MD, k * 256)
            dst[:, pl.ds(pl.multiple_of(k * 256, 128), 256)] = g.astype(BF16)

        if o != 0:
            go(out_copies(o))

    def pass_on():
        arrived(out_copies(2))
        go(relays())

    def inner_down():
        arrived(out_copies(1) + out_copies(-1) + relays())

        @pl.loop(0, 4)
        def _(q):
            for r in range(0, MD, 128):
                cols = pl.ds(pl.multiple_of(q * Q, 128), Q)
                prod = gdown[q, r : r + 128, :].astype(F32) * wd[r : r + 128, cols].astype(F32)
                acc = jnp.sum(prod.reshape(16, 8, Q), axis=0)
                gwacc[1] += acc[:, 0:256] + acc[:, 256:512] + acc[:, 512:768]

    gwacc[...] = jnp.zeros_like(gwacc)
    pl.semaphore_wait(barrier, 10)
    go([quarter(1), quarter(3)])
    loads[4].wait()
    yt[0, pl.ds(pl.multiple_of(x * MD, 128), MD), tokens_of(z)] = ystage[:, MU:].T
    yd_x.full()
    yd_z[0].full()
    loads[2].wait()
    xd_y[0].full()
    go([quarter(2)])
    loads[0].wait()
    loads[1].wait()
    s_send(0)
    loads[5].wait()
    for s in range(0, MU, 384):
        yt[1, s : s + 384, tokens_of(z)] = ystage[:, s : s + 384].T
    arrived([quarter(1), quarter(3)])
    xd_y[1].full()
    yd_x.half()
    yd_z[1].full()
    xd_y[0].half()
    yd_z[0].half()
    s_z(0)
    xd_y[2].full()
    yd_z[2].full()
    loads[3].wait()
    xu_x.full()
    xd_y[1].half()
    yd_z[1].half()
    xd_y[0].done()
    yd_z[0].done()
    t_x(0)
    arrived([quarter(2)])
    xd_y[3].full()
    yd_x.done()
    yd_z[3].full()
    xd_y[2].half()
    yd_z[2].half()
    xd_y[1].done()
    yd_z[1].done()
    t_y(0)
    xu_x.half()
    xu_x.done()
    xu_y[0].full()
    yu_z[0].full()
    xd_y[3].half()
    yd_z[3].half()
    xd_y[2].done()
    yd_z[2].done()
    s_send(1)
    s_z(1)
    xu_y[1].full()
    yu_z[1].full()
    xd_y[3].done()
    yd_z[3].done()
    for r in yd_z:
        r.fin()
    xu_y[0].half()
    yu_z[0].half()
    down(2)
    t_x(1)
    down(1)
    down(-1)
    xu_y[2].full()
    yu_z[2].full()
    t_y(1)
    down(0)
    pass_on()
    xu_y[1].half()
    yu_z[1].half()
    xu_y[0].done()
    yu_z[0].done()
    yu_z[0].fin()
    up(0, 0)
    t_fin(1)
    xu_y[2].half()
    yu_z[2].half()
    xu_y[1].done()
    yu_z[1].done()
    yu_z[1].fin()
    up(0, 1)
    up(1, 1)
    up(1, 0)
    inner_down()
    xu_y[2].done()
    yu_z[2].done()
    up(0, 2)
    up(1, 2)
    yu_z[2].fin()
    up(2, 0)
    up(2, 1)
    up(2, 2)

    gw = jnp.concatenate(
        [lanes(jnp.sum(gwacc[k], axis=0, keepdims=True)) for k in range(2)], axis=1
    )
    c = put(f_x, 4, x, at_x, fs.at[0], fr.at[0], gw)
    gw = get(f_x, 4, c)
    c = put(f_y, 4, y, at_y, fs.at[1], fr.at[1], gw)
    gw = get(f_y, 4, c)
    tu, td = ru[...], rd[...]
    both = jnp.concatenate([gw, lanes(tu * tu), lanes(td * td)], axis=1)
    c = put(f_core, 2, core, at_core, fs.at[2], fr.at[2], both)
    both = get(f_core, 2, c)
    c = put(f_z, 4, z, at_z, fs.at[3], fr.at[3], both)
    both = get(f_z, 4, c)

    def total(k):
        return jnp.sum(both[:, k * 128 : k * 128 + 128], axis=1, keepdims=True)

    stores = []
    for k, (rref, t, w, out) in enumerate(((ru, tu, wu, ou), (rd, td, wd, od))):
        inner = total(k)
        sigma = jnp.sqrt(total(2 + k) + 1e-06)
        v = t / sigma
        rref[...] = v
        gg[:, k * 128 : k * 128 + 128] = jnp.broadcast_to(inner / sigma, (1, 128))
        first = gain[k] / sigma
        second = gain[k] * inner / (sigma * sigma)

        if k == 0:

            @pl.loop(0, MU // 128)
            def _(r):
                rows = pl.ds(pl.multiple_of(r * 128, 128), 128)
                u = ucol[rows, :] * second
                for c0 in range(0, NU, 128):
                    cols = pl.ds(c0, 128)
                    w[rows, cols] = (first * gu[rows, cols] - u * v[:, c0 : c0 + 128]).astype(BF16)

        else:

            @pl.loop(0, MD // 128)
            def _(r):
                rows = pl.ds(pl.multiple_of(r * 128, 128), 128)
                u = ucol[pl.ds(pl.multiple_of(MU + r * 128, 128), 128), :] * second
                for q in range(4):
                    for c0 in range(0, Q, 128):
                        n0 = q * Q + c0
                        g = gdown[q, rows, c0 : c0 + 128].astype(F32)
                        w[rows, n0 : n0 + 128] = (first * g - u * v[:, n0 : n0 + 128]).astype(BF16)

        c = pltpu.make_async_copy(w, out, store_sem.at[k])
        c.start()
        stores.append(c)
    for c in sent:
        c.wait_send()
    for c in stores:
        c.wait()


def local(gain_pair, weight_up, weight_down, inputs_up, grads_up, inputs_down, grads_down, vector_up, vector_down):
    hbm = pl.BlockSpec(memory_space=pl.ANY)
    vmem = pl.BlockSpec(memory_space=pltpu.VMEM)
    dma = pltpu.SemaphoreType.DMA
    ou, od, gg, lu, ru, ld, rd = pl.pallas_call(
        kernel,
        out_shape=(
            jax.ShapeDtypeStruct((MU, NU), BF16),
            jax.ShapeDtypeStruct((MD, ND), BF16),
            jax.ShapeDtypeStruct((1, 256), F32),
            jax.ShapeDtypeStruct((1, MU), F32),
            jax.ShapeDtypeStruct((1, NU), F32),
            jax.ShapeDtypeStruct((1, MD), F32),
            jax.ShapeDtypeStruct((1, ND), F32),
        ),
        in_specs=[pl.BlockSpec(memory_space=pltpu.SMEM)] + [hbm] * 6 + [vmem] * 2,
        out_specs=(hbm, hbm) + (vmem,) * 5,
        scratch_shapes=[
            pltpu.VMEM((4, 4, TOK, NU), BF16),
            pltpu.VMEM((4, 4, TOK, Q), BF16),
            pltpu.VMEM((2, MU, T), BF16),
            pltpu.VMEM((TC, MALL), BF16),
            pltpu.VMEM((MU, NU), BF16),
            pltpu.VMEM((MD, ND), BF16),
            pltpu.VMEM((MU, NU), F32),
            pltpu.VMEM((3, MD, Q), BF16),
            pltpu.VMEM((4, MD, Q), BF16),
            pltpu.VMEM((2, MD // 2, Q), BF16),
            pltpu.VMEM((2, 8, 256), F32),
            pltpu.VMEM((MALL, 128), F32),
            pltpu.VMEM((ITERS, 2, 1, MALL), F32),
            pltpu.VMEM((ITERS, 4, 1, MALL), F32),
            pltpu.VMEM((ITERS, 4, 1, NALL + 256), F32),
            pltpu.VMEM((ITERS, 4, 1, NALL + 256), F32),
            pltpu.VMEM((2, 1, 512), F32),
            pltpu.VMEM((4, 1, 512), F32),
            pltpu.VMEM((4, 1, 256), F32),
            pltpu.VMEM((4, 1, 256), F32),
            dma((6,)),
            dma((2,)),
            dma((3,)),
            dma((3,)),
            dma((2, 4)),
            dma((2, 4)),
            dma((7, 4)),
            dma((7, 4)),
            dma((7, 8)),
            dma((7, 8)),
            dma((6,)),
            dma((6,)),
            dma((ITERS, 4, 3)),
            dma((ITERS, 4, 3)),
            dma((4, 3)),
            dma((4, 3)),
        ],
        compiler_params=pltpu.CompilerParams(
            collective_id=0, has_side_effects=True, vmem_limit_bytes=66 * 1024 * 1024 - 3 * 1024 * 1024
        ),
    )(
        gain_pair, weight_up, weight_down, inputs_up, grads_up, inputs_down, grads_down,
        vector_up.reshape(1, NU), vector_down.reshape(1, ND),
    )
    return (
        ou, od, jnp.stack([gg[0, 0], gg[0, 128]]),
        lu.reshape(MU), ru.reshape(NU), ld.reshape(MD), rd.reshape(ND),
    )


def solution(mesh):
    in_specs = (
        P(), P("row", "col"), P("row", "col"), P("row", "col"), P("col", "row"),
        P("row", "col"), P("col", "row"), P("col"), P("col"),
    )
    out_specs = (P("row", "col"), P("row", "col"), P(), P("row"), P("col"), P("row"), P("col"))
    return jax.shard_map(local, mesh=mesh, in_specs=in_specs, out_specs=out_specs, check_vma=False)
```

```python
import jax
import jax.numpy as jnp
from jax import lax
from jax.experimental import pallas as pl
from jax.experimental.pallas import tpu as pltpu
from jax.sharding import PartitionSpec as P

ITERS = 2
MESH = pl.DeviceIdType.MESH
F32 = jnp.float32
BF16 = jnp.bfloat16

TOK = 192
MU, MD = 1536, 384
NU, ND = 768, 3072
T = 3072
TC = 384
NALL = NU + ND
MALL = MU + MD
Q = ND // 4


def shift(i, d, n):
    return lax.rem(i + (d + n), n)


def lanes(v):
    total = v[:, 0:128]
    for k in range(128, v.shape[1], 128):
        total = total + v[:, k : k + 128]
    return total


def kernel(
    wu_h, wd_h, xu_h, yu_h, xd_h, yd_h, vu_in, vd_in,
    gu, gdown, ucol, urow, trow, sums,
    xu, xd, yt, ystage, wu, wd, gsend, relay, gwacc,
    e_core, e_z, e_x, e_y, f_t, f_x, f_y, f_c,
    load_sem, as_, ar, xs, xr, ys, yr, zs, zr, os_, or_, es, er, fs, fr,
):
    row = lax.axis_index("row")
    col = lax.axis_index("col")
    y, x = lax.div(row, 4), lax.rem(row, 4)
    z, core = lax.div(col, 2), lax.rem(col, 2)

    def at_x(i):
        return {"row": y * 4 + i, "col": col}

    def at_y(i):
        return {"row": i * 4 + x, "col": col}

    def at_z(i):
        return {"row": row, "col": i * 2 + core}

    def at_core(i):
        return {"row": row, "col": z * 2 + i}

    def at_col(i):
        return {"row": row, "col": i}

    barrier = pltpu.get_barrier_semaphore()
    for d in (1, 2, 3):
        pl.semaphore_signal(barrier, inc=1, device_id=at_x(shift(x, d, 4)), device_id_type=MESH)
        pl.semaphore_signal(barrier, inc=1, device_id=at_y(shift(y, d, 4)), device_id_type=MESH)
    for d in range(1, 8):
        pl.semaphore_signal(barrier, inc=1, device_id=at_col(shift(col, d, 8)), device_id_type=MESH)

    def half_rows(start, size, part):
        return pl.ds(start, size) if part is None else pl.ds(start + part * (size // 2), size // 2)

    def own_half(part):
        return pl.ds(0, TOK) if part is None else pl.ds(part * (TOK // 2), TOK // 2)

    def slots(part):
        return pl.ds(0, 4) if part is None else pl.ds(part * 2, 2)

    def tokens_of(i):
        return pl.ds(pl.multiple_of((i * 2 + core) * TC, 128), TC)

    loads = [
        pltpu.make_async_copy(wu_h, wu, load_sem.at[0]),
        pltpu.make_async_copy(wd_h, wd, load_sem.at[1]),
        pltpu.make_async_copy(xd_h.at[:, pl.ds(pl.multiple_of(x * Q, 128), Q)], xd.at[y, x], load_sem.at[2]),
        pltpu.make_async_copy(xu_h, xu.at[y, x], load_sem.at[3]),
        pltpu.make_async_copy(yd_h, ystage.at[:, pl.ds(MU, MD)], load_sem.at[4]),
        pltpu.make_async_copy(yu_h, ystage.at[:, pl.ds(0, MU)], load_sem.at[5]),
    ]
    for c in (4, 2, 5, 0, 1, 3):
        loads[c].start()

    sent = []

    def remote(ref, dst_ref, send, recv, device):
        return pltpu.make_async_remote_copy(
            src_ref=ref, dst_ref=dst_ref, send_sem=send, recv_sem=recv,
            device_id=device, device_id_type=MESH,
        )

    def go(copies):
        for c in copies:
            c.start()
            sent.append(c)

    def arrived(copies):
        for c in copies:
            c.wait_recv()

    class Ring:
        def __init__(self, me, where, region, send, recv, other=None):
            up, down = where(shift(me, 1, 4)), where(shift(me, -1, 4))

            def copy(o, part, device, k):
                ref = region(o, part)
                return remote(ref, ref, send.at[k], recv.at[k], device)

            self.a = lambda: [copy(0, None, up, 0), copy(0, None, down, 1)]
            self.b = lambda: [copy(-1, 0, up, 2), copy(1, 1, down, 3)]
            self.to_other = lambda k: copy((0, -1, 1, 2)[k], None, other, 4 + k)
            self.other = other is not None

        def full(self):
            go(self.a())
            if self.other:
                go([self.to_other(0)])

        def half(self):
            arrived(self.a())
            go(self.b())
            if self.other:
                go([self.to_other(1), self.to_other(2)])

        def done(self):
            arrived(self.b())
            if self.other:
                go([self.to_other(3)])

        def fin(self):
            arrived([self.to_other(k) for k in range(4)])

    def quarter(d):
        q = shift(x, d, 4)
        return remote(
            xd_h.at[:, pl.ds(pl.multiple_of(q * Q, 128), Q)], xd.at[y, x], as_.at[d - 1], ar.at[d - 1], at_x(q)
        )

    offs = (0, -1, 1, 2)
    xd_y = [
        Ring(y, at_y, lambda o, part, s=s: xd.at[shift(y, o, 4), shift(x, s, 4), own_half(part)], ys.at[k], yr.at[k])
        for k, s in enumerate(offs)
    ]
    xu_x = Ring(x, at_x, lambda o, part: xu.at[y, shift(x, o, 4), own_half(part)], xs.at[0], xr.at[0])
    xu_y = [
        Ring(
            y, at_y, lambda o, part, j=j: xu.at[shift(y, o, 4), slots(part), :, pl.ds(j * 256, 256)],
            ys.at[4 + j], yr.at[4 + j],
        )
        for j in range(3)
    ]

    yd_x = Ring(
        x, at_x,
        lambda o, part: yt.at[0, half_rows(shift(x, o, 4) * MD, MD, part), tokens_of(z)],
        xs.at[1], xr.at[1],
    )
    other = at_core(1 - core)
    yd_z = [
        Ring(
            z, at_z,
            lambda o, part, s=s: yt.at[0, half_rows(shift(x, s, 4) * MD, MD, part), tokens_of(shift(z, o, 4))],
            zs.at[k], zr.at[k], other,
        )
        for k, s in enumerate(offs)
    ]
    yu_z = [
        Ring(
            z, at_z, lambda o, part, j=j: yt.at[1, half_rows(j * 512, 512, part), tokens_of(shift(z, o, 4))],
            zs.at[4 + j], zr.at[4 + j], other,
        )
        for j in range(3)
    ]

    def xchg(buf, n, me, where, send, recv):
        return [
            remote(buf.at[me], buf.at[me], send.at[d - 1], recv.at[d - 1], where(shift(me, d, n)))
            for d in range(1, n)
        ]

    def put(buf, n, me, where, send, recv, value):
        buf[me] = value
        copies = xchg(buf, n, me, where, send, recv)
        for c in copies:
            c.start()
            sent.append(c)
        return copies

    def get(buf, n, copies):
        for c in copies:
            c.wait_recv()
        total = buf[0]
        for k in range(1, n):
            total = total + buf[k]
        return total

    def rows16(v):
        return jnp.broadcast_to(v, (16, v.shape[1])).astype(BF16)

    state = {"vu": None, "vd": None}

    def s_send(it):
        if it == 0:
            vu, vd = vu_in[...].reshape(1, NU), vd_in[...].reshape(1, ND)
        else:
            vu, vd = t_fin(it - 1)
        nt = (((1,), (1,)), ((), ()))
        su = lax.dot_general(rows16(vu), wu[...], nt, preferred_element_type=F32)[0:1]
        sd = lax.dot_general(rows16(vd), wd[...], nt, preferred_element_type=F32)[0:1]
        state["c"] = put(
            e_core.at[it], 2, core, at_core, es.at[it, 0], er.at[it, 0],
            jnp.concatenate([su, sd], axis=1),
        )

    def s_z(it):
        v = get(e_core.at[it], 2, state["c"])
        state["c"] = put(e_z.at[it], 4, z, at_z, es.at[it, 1], er.at[it, 1], v)

    def t_x(it):
        s = get(e_z.at[it], 4, state["c"])
        su, sd = s[:, :MU], s[:, MU:]
        state["s"] = (su, sd)
        tu = jnp.dot(rows16(su), wu[...], preferred_element_type=F32)[0:1]
        td = jnp.dot(rows16(sd), wd[...], preferred_element_type=F32)[0:1]
        v = jnp.concatenate([tu, td, lanes(su * su), lanes(sd * sd)], axis=1)
        state["c"] = put(e_x.at[it], 4, x, at_x, es.at[it, 2], er.at[it, 2], v)

    def t_y(it):
        v = get(e_x.at[it], 4, state["c"])
        state["c"] = put(e_y.at[it], 4, y, at_y, es.at[it, 3], er.at[it, 3], v)

    def t_fin(it):
        v = get(e_y.at[it], 4, state["c"])
        nu = jnp.sqrt(jnp.sum(v[:, NALL : NALL + 128], axis=1, keepdims=True) + 1e-06)
        nd = jnp.sqrt(jnp.sum(v[:, NALL + 128 :], axis=1, keepdims=True) + 1e-06)
        tu, td = v[:, :NU] / nu, v[:, NU:NALL] / nd
        if it + 1 == ITERS:
            su, sd = state["s"]
            uu, ud = su / nu, sd / nd
            u = jnp.concatenate([uu, ud], axis=1)
            urow[...] = u
            trow[...] = jnp.concatenate([tu, td], axis=1)
            ub = u.astype(BF16).astype(F32)
            for s in range(0, MALL, 128):
                ucol[s : s + 128, :] = jnp.broadcast_to(ub[:, s : s + 128], (128, 128)).T
            squares = jnp.concatenate([lanes(tu * tu), lanes(td * td)], axis=1)
            state["t"] = put(f_t, 8, col, at_col, fs.at[3], fr.at[3], squares)
        return tu, td

    def product(which, xref, m0, tm, n0):
        xs_ = xref[:, :, :, pl.ds(pl.multiple_of(n0, 128), 256)].reshape(T, 256)
        return jnp.dot(yt[which, pl.ds(pl.multiple_of(m0, 128), tm), :], xs_, preferred_element_type=F32)

    def up(m, n):
        @pl.loop(0, 2)
        def _(k):
            rows, cols = pl.ds(pl.multiple_of(m * 512 + k * 256, 128), 256), pl.ds(n * 256, 256)
            g = product(1, xu, m * 512 + k * 256, 256, n * 256)
            gu[rows, cols] = g
            prod = g * wu[rows, cols].astype(F32)
            gwacc[0] += jnp.sum(prod.reshape(32, 8, 256), axis=0)

    def out_copies(o):
        if o == 2:
            return [
                remote(gsend.at[0, pl.ds(0, 192)], relay.at[0], os_.at[0], or_.at[0], at_x(shift(x, 1, 4))),
                remote(gsend.at[0, pl.ds(192, 192)], relay.at[1], os_.at[1], or_.at[1], at_x(shift(x, -1, 4))),
            ]
        k = 2 if o == 1 else 3
        return [remote(gsend.at[k - 1], gdown.at[x], os_.at[k], or_.at[k], at_x(shift(x, o, 4)))]

    def relays():
        return [
            remote(relay.at[0], gdown.at[shift(x, -1, 4), pl.ds(0, 192)], os_.at[4], or_.at[4], at_x(shift(x, 1, 4))),
            remote(relay.at[1], gdown.at[shift(x, 1, 4), pl.ds(192, 192)], os_.at[5], or_.at[5], at_x(shift(x, -1, 4))),
        ]

    def down(o):
        dst = gdown.at[x] if o == 0 else gsend.at[{2: 0, 1: 1, -1: 2}[o]]

        @pl.loop(0, Q // 256)
        def _(k):
            g = product(0, xd, shift(x, o, 4) * MD, MD, k * 256)
            dst[:, pl.ds(pl.multiple_of(k * 256, 128), 256)] = g.astype(BF16)

        if o != 0:
            go(out_copies(o))

    def pass_on():
        arrived(out_copies(2))
        go(relays())

    def inner_down():
        arrived(out_copies(1) + out_copies(-1) + relays())

        @pl.loop(0, 4)
        def _(q):
            for r in range(0, MD, 128):
                cols = pl.ds(pl.multiple_of(q * Q, 128), Q)
                prod = gdown[q, r : r + 128, :].astype(F32) * wd[r : r + 128, cols].astype(F32)
                acc = jnp.sum(prod.reshape(16, 8, Q), axis=0)
                gwacc[1] += acc[:, 0:256] + acc[:, 256:512] + acc[:, 512:768]

    gwacc[...] = jnp.zeros_like(gwacc)
    pl.semaphore_wait(barrier, 13)
    go([quarter(1), quarter(3)])
    loads[4].wait()
    yt[0, pl.ds(pl.multiple_of(x * MD, 128), MD), tokens_of(z)] = ystage[:, MU:].T
    yd_x.full()
    yd_z[0].full()
    loads[2].wait()
    xd_y[0].full()
    go([quarter(2)])
    loads[0].wait()
    loads[1].wait()
    s_send(0)
    loads[5].wait()
    for s in range(0, MU, 384):
        yt[1, s : s + 384, tokens_of(z)] = ystage[:, s : s + 384].T
    arrived([quarter(1), quarter(3)])
    xd_y[1].full()
    yd_x.half()
    yd_z[1].full()
    xd_y[0].half()
    yd_z[0].half()
    s_z(0)
    xd_y[2].full()
    yd_z[2].full()
    loads[3].wait()
    xu_x.full()
    xd_y[1].half()
    yd_z[1].half()
    xd_y[0].done()
    yd_z[0].done()
    t_x(0)
    arrived([quarter(2)])
    xd_y[3].full()
    yd_x.done()
    yd_z[3].full()
    xd_y[2].half()
    yd_z[2].half()
    xd_y[1].done()
    yd_z[1].done()
    t_y(0)
    xu_x.half()
    xu_x.done()
    xu_y[0].full()
    yu_z[0].full()
    xd_y[3].half()
    yd_z[3].half()
    xd_y[2].done()
    yd_z[2].done()
    s_send(1)
    s_z(1)
    xu_y[1].full()
    yu_z[1].full()
    xd_y[3].done()
    yd_z[3].done()
    for r in yd_z:
        r.fin()
    xu_y[0].half()
    yu_z[0].half()
    down(2)
    t_x(1)
    down(1)
    down(-1)
    xu_y[2].full()
    yu_z[2].full()
    t_y(1)
    down(0)
    pass_on()
    xu_y[1].half()
    yu_z[1].half()
    xu_y[0].done()
    yu_z[0].done()
    yu_z[0].fin()
    up(0, 0)
    t_fin(1)
    xu_y[2].half()
    yu_z[2].half()
    xu_y[1].done()
    yu_z[1].done()
    yu_z[1].fin()
    up(0, 1)
    up(1, 1)
    up(1, 0)
    inner_down()
    xu_y[2].done()
    yu_z[2].done()
    up(0, 2)
    up(1, 2)
    yu_z[2].fin()
    up(2, 0)
    up(2, 1)
    up(2, 2)

    squares = get(f_t, 8, state["t"])
    gw = jnp.concatenate(
        [lanes(jnp.sum(gwacc[k], axis=0, keepdims=True)) for k in range(2)], axis=1
    )
    for k, (buf, n, me, where) in enumerate(((f_x, 4, x, at_x), (f_y, 4, y, at_y), (f_c, 8, col, at_col))):
        gw = get(buf, n, put(buf, n, me, where, fs.at[k], fr.at[k], gw))
    sums[...] = jnp.concatenate([gw, squares], axis=1)
    for c in sent:
        c.wait_send()


def scale(gain, gu, gdown, ucol, urow, trow, sums, ou, od, gg, lu, ru, ld, rd, su, sd, sem):
    def total(k):
        return jnp.sum(sums[:, k * 128 : k * 128 + 128], axis=1, keepdims=True)

    def factors(k):
        inner = total(k)
        sigma = jnp.sqrt(total(2 + k) + 1e-06)
        gg[k] = (inner / sigma)[0, 0]
        return sigma, gain[k] / sigma, gain[k] * inner / (sigma * sigma)

    stores = []

    def store(src, dst):
        c = pltpu.make_async_copy(src, dst, sem.at[len(stores)])
        c.start()
        stores.append(c)

    sigma, first, second = factors(0)
    v = trow[:, :NU] / sigma
    ru[...] = v.reshape(NU)
    lu[...] = urow[:, :MU].reshape(MU)
    for r0 in range(0, MU, 384):

        @pl.loop(0, 3)
        def _(r):
            rows = pl.ds(pl.multiple_of(r0 + r * 128, 128), 128)
            u = ucol[rows, :] * second
            for c0 in range(0, NU, 128):
                cols = pl.ds(c0, 128)
                su[rows, cols] = (first * gu[rows, cols] - u * v[:, c0 : c0 + 128]).astype(BF16)

        store(su.at[pl.ds(r0, 384)], ou.at[pl.ds(r0, 384)])

    sigma, first, second = factors(1)
    v = trow[:, NU:] / sigma
    rd[...] = v.reshape(ND)
    ld[...] = urow[:, MU:].reshape(MD)
    for r0 in range(0, MD, 128):
        rows = pl.ds(r0, 128)
        u = ucol[MU + r0 : MU + r0 + 128, :] * second
        for n0 in range(0, ND, 128):
            g = gdown[n0 // Q, rows, n0 % Q : n0 % Q + 128].astype(F32)
            sd[rows, n0 : n0 + 128] = (first * g - u * v[:, n0 : n0 + 128]).astype(BF16)
        store(sd.at[rows], od.at[rows])
    for c in stores:
        c.wait()


def local(gain_pair, weight_up, weight_down, inputs_up, grads_up, inputs_down, grads_down, vector_up, vector_down):
    hbm = pl.BlockSpec(memory_space=pl.ANY)
    vmem = pl.BlockSpec(memory_space=pltpu.VMEM)
    smem = pl.BlockSpec(memory_space=pltpu.SMEM)
    dma = pltpu.SemaphoreType.DMA
    parts = pl.pallas_call(
        kernel,
        out_shape=(
            pltpu.VMEM((MU, NU), F32),
            pltpu.VMEM((4, MD, Q), BF16),
            pltpu.VMEM((MALL, 128), F32),
            pltpu.VMEM((1, MALL), F32),
            pltpu.VMEM((1, NALL), F32),
            pltpu.VMEM((1, 512), F32),
        ),
        in_specs=[hbm] * 6 + [vmem] * 2,
        out_specs=(vmem,) * 6,
        scratch_shapes=[
            pltpu.VMEM((4, 4, TOK, NU), BF16),
            pltpu.VMEM((4, 4, TOK, Q), BF16),
            pltpu.VMEM((2, MU, T), BF16),
            pltpu.VMEM((TC, MALL), BF16),
            pltpu.VMEM((MU, NU), BF16),
            pltpu.VMEM((MD, ND), BF16),
            pltpu.VMEM((3, MD, Q), BF16),
            pltpu.VMEM((2, MD // 2, Q), BF16),
            pltpu.VMEM((2, 8, 256), F32),
            pltpu.VMEM((ITERS, 2, 1, MALL), F32),
            pltpu.VMEM((ITERS, 4, 1, MALL), F32),
            pltpu.VMEM((ITERS, 4, 1, NALL + 256), F32),
            pltpu.VMEM((ITERS, 4, 1, NALL + 256), F32),
            pltpu.VMEM((8, 1, 256), F32),
            pltpu.VMEM((4, 1, 256), F32),
            pltpu.VMEM((4, 1, 256), F32),
            pltpu.VMEM((8, 1, 256), F32),
            dma((6,)),
            dma((3,)),
            dma((3,)),
            dma((2, 4)),
            dma((2, 4)),
            dma((7, 4)),
            dma((7, 4)),
            dma((7, 8)),
            dma((7, 8)),
            dma((6,)),
            dma((6,)),
            dma((ITERS, 4, 3)),
            dma((ITERS, 4, 3)),
            dma((4, 7)),
            dma((4, 7)),
        ],
        compiler_params=pltpu.CompilerParams(
            collective_id=0, has_side_effects=True, vmem_limit_bytes=48 * 1024 * 1024
        ),
    )(weight_up, weight_down, inputs_up, grads_up, inputs_down, grads_down, vector_up, vector_down)
    return tuple(
        pl.pallas_call(
            scale,
            out_shape=(
                jax.ShapeDtypeStruct((MU, NU), BF16),
                jax.ShapeDtypeStruct((MD, ND), BF16),
                jax.ShapeDtypeStruct((2,), F32),
                jax.ShapeDtypeStruct((MU,), F32),
                jax.ShapeDtypeStruct((NU,), F32),
                jax.ShapeDtypeStruct((MD,), F32),
                jax.ShapeDtypeStruct((ND,), F32),
            ),
            in_specs=[smem] + [vmem] * 6,
            out_specs=(hbm, hbm, smem) + (vmem,) * 4,
            scratch_shapes=[
                pltpu.VMEM((MU, NU), BF16),
                pltpu.VMEM((MD, ND), BF16),
                dma((7,)),
            ],
            compiler_params=pltpu.CompilerParams(vmem_limit_bytes=24 * 1024 * 1024),
        )(gain_pair, *parts)
    )


def solution(mesh):
    in_specs = (
        P(), P("row", "col"), P("row", "col"), P("row", "col"), P("col", "row"),
        P("row", "col"), P("col", "row"), P("col"), P("col"),
    )
    out_specs = (P("row", "col"), P("row", "col"), P(), P("row"), P("col"), P("row"), P("col"))
    return jax.shard_map(local, mesh=mesh, in_specs=in_specs, out_specs=out_specs, check_vma=False)
```

```python
import jax
import jax.numpy as jnp
from jax import lax
from jax.experimental import pallas as pl
from jax.experimental.pallas import tpu as pltpu
from jax.sharding import PartitionSpec as P

ITERS = 2
MESH = pl.DeviceIdType.MESH
F32 = jnp.float32
BF16 = jnp.bfloat16

TOK = 192
MU, MD = 1536, 384
NU, ND = 768, 3072
T = 3072
TC = 384
NALL = NU + ND
MALL = MU + MD
Q = ND // 4
UP_GROUPS = ((0, 512), (512, 512), (1024, 384), (1408, 128))
XFIRST = 256
ORDER = (
    "q13", "by_f", "dz_f", "xd0_f", "turnU", "dw0_f", "zu0_f", "dz_h", "s_send0", "ydx_f", "q13w", "xd2_f",
    "zu3_f", "dw0_h", "s_z0", "by_h", "dw2_f", "xd1_f", "ydx_h", "q2", "zd1_f", "dz_d", "dw0_d", "xd2_h",
    "zu0_h", "dw1_f", "zu3_h", "by_d", "ydx_d", "t_x0", "zd1_h", "q2f", "zd3_f", "dw1_h", "xd0_h", "dw2_h",
    "t_y0", "q2w", "xd3_f", "xux_f", "zu0_d", "zu3_d", "dw3_f", "zu2_f", "xd2_d", "dw1_d", "s_send1", "zd1_d",
    "xd1_h", "zd3_h", "xux_h", "dw2_d", "dw3_h", "s_z1", "xd3_h", "bx_f", "dw0_n", "dw1_n", "zd2_f", "zd3_d",
    "zd1_n", "xux_d", "yu0_f", "zd0_f", "t_x1", "dw3_d", "xd0_d", "dw2_n", "xd1_d", "zd3_n", "zd2_h", "zu0_n",
    "xd3_d", "dw3_n", "zu2_h", "zu3_n", "yu1_f", "bx_h", "down2", "zd2_d", "zd0_h", "zu1_f", "down3", "bx_d",
    "zu2_d", "t_y1", "yu0_h", "zd2_n", "down1", "zd0_d", "up0_2", "yu1_h", "zu2_n", "t_fin1", "up3_2",
    "up2_2", "zd0_n", "pass_on", "yu0_d", "up3_0", "zu1_h", "down0", "up0_0", "yu1_d", "up3_1", "zu1_d",
    "up2_1", "up2_0", "up0_1", "zu1_n", "up1_2", "up1_1", "up1_0", "inner_down",
)


def shift(i, d, n):
    return lax.rem(i + (d + n), n)


def lanes(v):
    total = v[:, 0:128]
    for k in range(128, v.shape[1], 128):
        total = total + v[:, k : k + 128]
    return total


def kernel(
    wu_h, wd_h, xu_h, yu_h, xd_h, yd_h, vu_in, vd_in,
    gu, gdown, ucol, urow, trow, sums,
    xu, xd, yt, ystage, wu, wd, gsend, relay, qrelay, gwacc,
    e_core, e_z, e_x, e_y, f_t, f_x, f_y, f_c,
    load_sem, as_, ar, xs, xr, ys, yr, zs, zr, os_, or_, es, er, fs, fr,
):
    row = lax.axis_index("row")
    col = lax.axis_index("col")
    y, x = lax.div(row, 4), lax.rem(row, 4)
    z, core = lax.div(col, 2), lax.rem(col, 2)

    def at_x(i):
        return {"row": y * 4 + i, "col": col}

    def at_y(i):
        return {"row": i * 4 + x, "col": col}

    def at_z(i):
        return {"row": row, "col": i * 2 + core}

    def at_core(i):
        return {"row": row, "col": z * 2 + i}

    def at_col(i):
        return {"row": row, "col": i}

    barrier = pltpu.get_barrier_semaphore()
    for d in (1, 2, 3):
        pl.semaphore_signal(barrier, inc=1, device_id=at_x(shift(x, d, 4)), device_id_type=MESH)
        pl.semaphore_signal(barrier, inc=1, device_id=at_y(shift(y, d, 4)), device_id_type=MESH)
    for d in range(1, 8):
        pl.semaphore_signal(barrier, inc=1, device_id=at_col(shift(col, d, 8)), device_id_type=MESH)

    def half_rows(start, size, part):
        return pl.ds(start, size) if part is None else pl.ds(start + part * (size // 2), size // 2)

    def own_half(part):
        return pl.ds(0, TOK) if part is None else pl.ds(part * (TOK // 2), TOK // 2)

    def slots(part):
        return pl.ds(0, 4) if part is None else pl.ds(part * 2, 2)

    def tokens_of(i):
        return pl.ds(pl.multiple_of((i * 2 + core) * TC, 128), TC)

    loads = [
        pltpu.make_async_copy(wu_h, wu, load_sem.at[0]),
        pltpu.make_async_copy(wd_h, wd, load_sem.at[1]),
        pltpu.make_async_copy(xd_h.at[:, pl.ds(pl.multiple_of(x * Q, 128), Q)], xd.at[y, x], load_sem.at[2]),
        pltpu.make_async_copy(xu_h, xu.at[y, x], load_sem.at[3]),
        pltpu.make_async_copy(yd_h, ystage.at[:, pl.ds(MU, MD)], load_sem.at[4]),
        pltpu.make_async_copy(yu_h, ystage.at[:, pl.ds(0, MU)], load_sem.at[5]),
    ]
    for c in (4, 2, 5, 0, 1, 3):
        loads[c].start()

    sent = []

    def remote(ref, dst_ref, send, recv, device):
        return pltpu.make_async_remote_copy(
            src_ref=ref, dst_ref=dst_ref, send_sem=send, recv_sem=recv,
            device_id=device, device_id_type=MESH,
        )

    def go(copies):
        for c in copies:
            c.start()
            sent.append(c)

    def arrived(copies):
        for c in copies:
            c.wait_recv()

    class Ring:
        def __init__(self, me, where, region, send, recv, other=None):
            up, down = where(shift(me, 1, 4)), where(shift(me, -1, 4))

            def copy(o, part, device, k):
                ref = region(o, part)
                return remote(ref, ref, send.at[k], recv.at[k], device)

            self.a = lambda: [copy(0, None, up, 0), copy(0, None, down, 1)]
            self.b = lambda: [copy(-1, 0, up, 2), copy(1, 1, down, 3)]
            self.to_other = lambda k: copy((0, -1, 1, 2)[k], None, other, 4 + k)
            self.other = other is not None

        def full(self):
            go(self.a())
            if self.other:
                go([self.to_other(0)])

        def half(self):
            arrived(self.a())
            go(self.b())
            if self.other:
                go([self.to_other(1), self.to_other(2)])

        def done(self):
            arrived(self.b())
            if self.other:
                go([self.to_other(3)])

        def fin(self):
            arrived([self.to_other(k) for k in range(4)])

    def quarter(d):
        q = shift(x, d, 4)
        return remote(
            xd_h.at[:, pl.ds(pl.multiple_of(q * Q, 128), Q)], xd.at[y, x], as_.at[d - 1], ar.at[d - 1], at_x(q)
        )

    def far_quarter():
        cols = pl.ds(pl.multiple_of(shift(x, 2, 4) * Q, 128), Q)
        return [
            remote(xd_h.at[own_half(k), cols], qrelay.at[k], as_.at[k + 3], ar.at[k + 3], at_x(shift(x, d, 4)))
            for k, d in enumerate((1, -1))
        ]

    def far_quarter_relays():
        return [
            remote(
                qrelay.at[k], xd.at[y, shift(x, -d, 4), own_half(k)], as_.at[k + 5], ar.at[k + 5], at_x(shift(x, d, 4))
            )
            for k, d in enumerate((1, -1))
        ]

    def far_quarter_on():
        arrived(far_quarter())
        go(far_quarter_relays())

    offs = (0, -1, 1, 2)
    xd_y = [
        Ring(y, at_y, lambda o, part, s=s: xd.at[shift(y, o, 4), shift(x, s, 4), own_half(part)], ys.at[k], yr.at[k])
        for k, s in enumerate(offs)
    ]
    first_cols, last_cols = pl.ds(0, 512), pl.ds(512, 256)
    xu_x = Ring(x, at_x, lambda o, part: xu.at[y, shift(x, o, 4), own_half(part), first_cols], xs.at[0], xr.at[0])
    xu_y = [
        Ring(
            y, at_y, lambda o, part, j=j: xu.at[shift(y, o, 4), slots(part), :, pl.ds(j * 256, 256)],
            ys.at[4 + j], yr.at[4 + j],
        )
        for j in range(2)
    ]
    last_y = Ring(y, at_y, lambda o, part: xu.at[shift(y, o, 4), x, own_half(part), last_cols], ys.at[6], yr.at[6])
    last_x = Ring(x, at_x, lambda o, part: xu.at[slots(part), shift(x, o, 4), :, last_cols], xs.at[2], xr.at[2])

    yd_x = Ring(
        x, at_x,
        lambda o, part: yt.at[0, half_rows(shift(x, o, 4) * MD, XFIRST, part), tokens_of(z)],
        xs.at[1], xr.at[1],
    )
    other = at_core(1 - core)
    yd_z = [
        Ring(
            z, at_z,
            lambda o, part, s=s: yt.at[0, half_rows(shift(x, s, 4) * MD, XFIRST, part), tokens_of(shift(z, o, 4))],
            zs.at[k], zr.at[k], other,
        )
        for k, s in enumerate(offs)
    ]
    rest = MD - XFIRST
    rest_z = Ring(
        z, at_z,
        lambda o, part: yt.at[0, half_rows(x * MD + XFIRST, rest, part), tokens_of(shift(z, o, 4))],
        xs.at[3], xr.at[3],
    )
    rest_x = [
        Ring(
            x, at_x,
            lambda o, part, s=s: yt.at[0, half_rows(shift(x, o, 4) * MD + XFIRST, rest, part), tokens_of(shift(z, s, 4))],
            zs.at[8 + k], zr.at[8 + k], other,
        )
        for k, s in enumerate(offs)
    ]
    yu_z = [
        Ring(
            z, at_z,
            lambda o, part, m=m, n=n: yt.at[1, half_rows(m, n, part), tokens_of(shift(z, o, 4))],
            zs.at[4 + j], zr.at[4 + j], other,
        )
        for j, (m, n) in enumerate(UP_GROUPS)
    ]

    def xchg(buf, n, me, where, send, recv):
        return [
            remote(buf.at[me], buf.at[me], send.at[d - 1], recv.at[d - 1], where(shift(me, d, n)))
            for d in range(1, n)
        ]

    def put(buf, n, me, where, send, recv, value):
        buf[me] = value
        copies = xchg(buf, n, me, where, send, recv)
        for c in copies:
            c.start()
            sent.append(c)
        return copies

    def get(buf, n, copies):
        for c in copies:
            c.wait_recv()
        total = buf[0]
        for k in range(1, n):
            total = total + buf[k]
        return total

    def rows16(v):
        return jnp.broadcast_to(v, (16, v.shape[1])).astype(BF16)

    state = {"vu": None, "vd": None}

    def s_send(it):
        if it == 0:
            vu, vd = vu_in[...].reshape(1, NU), vd_in[...].reshape(1, ND)
        else:
            vu, vd = t_fin(it - 1)
        nt = (((1,), (1,)), ((), ()))
        su = lax.dot_general(rows16(vu), wu[...], nt, preferred_element_type=F32)[0:1]
        sd = lax.dot_general(rows16(vd), wd[...], nt, preferred_element_type=F32)[0:1]
        state["c"] = put(
            e_core.at[it], 2, core, at_core, es.at[it, 0], er.at[it, 0],
            jnp.concatenate([su, sd], axis=1),
        )

    def s_z(it):
        v = get(e_core.at[it], 2, state["c"])
        state["c"] = put(e_z.at[it], 4, z, at_z, es.at[it, 1], er.at[it, 1], v)

    def t_x(it):
        s = get(e_z.at[it], 4, state["c"])
        su, sd = s[:, :MU], s[:, MU:]
        state["s"] = (su, sd)
        tu = jnp.dot(rows16(su), wu[...], preferred_element_type=F32)[0:1]
        td = jnp.dot(rows16(sd), wd[...], preferred_element_type=F32)[0:1]
        v = jnp.concatenate([tu, td, lanes(su * su), lanes(sd * sd)], axis=1)
        state["c"] = put(e_x.at[it], 4, x, at_x, es.at[it, 2], er.at[it, 2], v)

    def t_y(it):
        v = get(e_x.at[it], 4, state["c"])
        state["c"] = put(e_y.at[it], 4, y, at_y, es.at[it, 3], er.at[it, 3], v)

    def t_fin(it):
        v = get(e_y.at[it], 4, state["c"])
        nu = jnp.sqrt(jnp.sum(v[:, NALL : NALL + 128], axis=1, keepdims=True) + 1e-06)
        nd = jnp.sqrt(jnp.sum(v[:, NALL + 128 :], axis=1, keepdims=True) + 1e-06)
        tu, td = v[:, :NU] / nu, v[:, NU:NALL] / nd
        if it + 1 == ITERS:
            su, sd = state["s"]
            uu, ud = su / nu, sd / nd
            u = jnp.concatenate([uu, ud], axis=1)
            urow[...] = u
            trow[...] = jnp.concatenate([tu, td], axis=1)
            ub = u.astype(BF16).astype(F32)
            for s in range(0, MALL, 128):
                ucol[s : s + 128, :] = jnp.broadcast_to(ub[:, s : s + 128], (128, 128)).T
            squares = jnp.concatenate([lanes(tu * tu), lanes(td * td)], axis=1)
            state["t"] = put(f_t, 8, col, at_col, fs.at[3], fr.at[3], squares)
        return tu, td

    def product(which, xref, m0, tm, n0):
        xs_ = xref[:, :, :, pl.ds(pl.multiple_of(n0, 128), 256)].reshape(T, 256)
        return jnp.dot(yt[which, pl.ds(pl.multiple_of(m0, 128), tm), :], xs_, preferred_element_type=F32)

    def up(j, n):
        start, size = UP_GROUPS[j]
        tm = 256 if size % 256 == 0 else size

        @pl.loop(0, size // tm)
        def _(k):
            rows, cols = pl.ds(pl.multiple_of(start + k * tm, 128), tm), pl.ds(n * 256, 256)
            g = product(1, xu, start + k * tm, tm, n * 256)
            gu[rows, cols] = g
            prod = g * wu[rows, cols].astype(F32)
            gwacc[0] += jnp.sum(prod.reshape(tm // 8, 8, 256), axis=0)

    def out_copies(o):
        if o == 2:
            return [
                remote(gsend.at[0, pl.ds(0, 192)], relay.at[0], os_.at[0], or_.at[0], at_x(shift(x, 1, 4))),
                remote(gsend.at[0, pl.ds(192, 192)], relay.at[1], os_.at[1], or_.at[1], at_x(shift(x, -1, 4))),
            ]
        k = 2 if o == 1 else 3
        return [remote(gsend.at[k - 1], gdown.at[x], os_.at[k], or_.at[k], at_x(shift(x, o, 4)))]

    def relays():
        return [
            remote(relay.at[0], gdown.at[shift(x, -1, 4), pl.ds(0, 192)], os_.at[4], or_.at[4], at_x(shift(x, 1, 4))),
            remote(relay.at[1], gdown.at[shift(x, 1, 4), pl.ds(192, 192)], os_.at[5], or_.at[5], at_x(shift(x, -1, 4))),
        ]

    def down(o):
        dst = gdown.at[x] if o == 0 else gsend.at[{2: 0, 1: 1, -1: 2}[o]]

        @pl.loop(0, Q // 256)
        def _(k):
            g = product(0, xd, shift(x, o, 4) * MD, MD, k * 256)
            dst[:, pl.ds(pl.multiple_of(k * 256, 128), 256)] = g.astype(BF16)

        if o != 0:
            go(out_copies(o))

    def pass_on():
        arrived(out_copies(2))
        go(relays())

    def inner_down():
        arrived(out_copies(1) + out_copies(-1) + relays())

        @pl.loop(0, 4)
        def _(q):
            for r in range(0, MD, 128):
                cols = pl.ds(pl.multiple_of(q * Q, 128), Q)
                prod = gdown[q, r : r + 128, :].astype(F32) * wd[r : r + 128, cols].astype(F32)
                acc = jnp.sum(prod.reshape(16, 8, Q), axis=0)
                gwacc[1] += acc[:, 0:256] + acc[:, 256:512] + acc[:, 512:768]

    gwacc[...] = jnp.zeros_like(gwacc)

    def loaded(*which):
        for k in which:
            loads[k].wait()

    def turn_down():
        loaded(4)
        yt[0, pl.ds(pl.multiple_of(x * MD, 128), MD), tokens_of(z)] = ystage[:, MU:].T

    def turn_up():
        loaded(5)
        for s in range(0, MU, 384):
            yt[1, s : s + 384, tokens_of(z)] = ystage[:, s : s + 384].T

    acts = {
        "q13": lambda: go([quarter(1), quarter(3)]),
        "q13w": lambda: arrived([quarter(1), quarter(3)]),
        "q2": lambda: go(far_quarter()),
        "q2f": far_quarter_on,
        "q2w": lambda: arrived(far_quarter_relays()),
        "turnU": turn_up,
        "pass_on": pass_on,
        "inner_down": inner_down,
    }
    for k, o in enumerate((0, 1, 2, -1)):
        acts[f"down{k}"] = lambda o=o: down(o)
    for j in range(len(UP_GROUPS)):
        for n in range(3):
            acts[f"up{j}_{n}"] = lambda j=j, n=n: up(j, n)
    for it in range(ITERS):
        acts[f"s_send{it}"] = lambda it=it: s_send(it)
        acts[f"s_z{it}"] = lambda it=it: s_z(it)
        acts[f"t_x{it}"] = lambda it=it: t_x(it)
        acts[f"t_y{it}"] = lambda it=it: t_y(it)
    acts["t_fin1"] = lambda: t_fin(1)
    rings = {"xux": xu_x, "ydx": yd_x, "by": last_y, "bx": last_x, "dz": rest_z}
    for name, group in (("xd", xd_y), ("yu", xu_y), ("zd", yd_z), ("zu", yu_z), ("dw", rest_x)):
        for k, r in enumerate(group):
            rings[f"{name}{k}"] = r
    for name, r in rings.items():
        acts[name + "_f"] = r.full
        acts[name + "_h"] = r.half
        acts[name + "_d"] = r.done
        acts[name + "_n"] = r.fin

    turn_down()
    loaded(2, 3)
    pl.semaphore_wait(barrier, 13)
    for name in ORDER:
        if name == "s_send0":
            loaded(0, 1)
        acts[name]()

    squares = get(f_t, 8, state["t"])
    gw = jnp.concatenate(
        [lanes(jnp.sum(gwacc[k], axis=0, keepdims=True)) for k in range(2)], axis=1
    )
    for k, (buf, n, me, where) in enumerate(((f_x, 4, x, at_x), (f_y, 4, y, at_y), (f_c, 8, col, at_col))):
        gw = get(buf, n, put(buf, n, me, where, fs.at[k], fr.at[k], gw))
    sums[...] = jnp.concatenate([gw, squares], axis=1)
    for c in sent:
        c.wait_send()


def scale(gain, gu, gdown, ucol, urow, trow, sums, ou, od, gg, lu, ru, ld, rd, su, sd, sem):
    def total(k):
        return jnp.sum(sums[:, k * 128 : k * 128 + 128], axis=1, keepdims=True)

    def factors(k):
        inner = total(k)
        sigma = jnp.sqrt(total(2 + k) + 1e-06)
        gg[k] = (inner / sigma)[0, 0]
        return sigma, gain[k] / sigma, gain[k] * inner / (sigma * sigma)

    stores = []

    def store(src, dst):
        c = pltpu.make_async_copy(src, dst, sem.at[len(stores)])
        c.start()
        stores.append(c)

    sigma, first, second = factors(0)
    v = trow[:, :NU] / sigma
    ru[...] = v.reshape(NU)
    lu[...] = urow[:, :MU].reshape(MU)
    for r0 in range(0, MU, 384):

        @pl.loop(0, 3)
        def _(r):
            rows = pl.ds(pl.multiple_of(r0 + r * 128, 128), 128)
            u = ucol[rows, :] * second
            for c0 in range(0, NU, 128):
                cols = pl.ds(c0, 128)
                su[rows, cols] = (first * gu[rows, cols] - u * v[:, c0 : c0 + 128]).astype(BF16)

        store(su.at[pl.ds(r0, 384)], ou.at[pl.ds(r0, 384)])

    sigma, first, second = factors(1)
    v = trow[:, NU:] / sigma
    rd[...] = v.reshape(ND)
    ld[...] = urow[:, MU:].reshape(MD)
    for r0 in range(0, MD, 128):
        rows = pl.ds(r0, 128)
        u = ucol[MU + r0 : MU + r0 + 128, :] * second
        for n0 in range(0, ND, 128):
            g = gdown[n0 // Q, rows, n0 % Q : n0 % Q + 128].astype(F32)
            sd[rows, n0 : n0 + 128] = (first * g - u * v[:, n0 : n0 + 128]).astype(BF16)
        store(sd.at[rows], od.at[rows])
    for c in stores:
        c.wait()


def local(gain_pair, weight_up, weight_down, inputs_up, grads_up, inputs_down, grads_down, vector_up, vector_down):
    hbm = pl.BlockSpec(memory_space=pl.ANY)
    vmem = pl.BlockSpec(memory_space=pltpu.VMEM)
    smem = pl.BlockSpec(memory_space=pltpu.SMEM)
    dma = pltpu.SemaphoreType.DMA
    parts = pl.pallas_call(
        kernel,
        out_shape=(
            pltpu.VMEM((MU, NU), F32),
            pltpu.VMEM((4, MD, Q), BF16),
            pltpu.VMEM((MALL, 128), F32),
            pltpu.VMEM((1, MALL), F32),
            pltpu.VMEM((1, NALL), F32),
            pltpu.VMEM((1, 512), F32),
        ),
        in_specs=[hbm] * 6 + [vmem] * 2,
        out_specs=(vmem,) * 6,
        scratch_shapes=[
            pltpu.VMEM((4, 4, TOK, NU), BF16),
            pltpu.VMEM((4, 4, TOK, Q), BF16),
            pltpu.VMEM((2, MU, T), BF16),
            pltpu.VMEM((TC, MALL), BF16),
            pltpu.VMEM((MU, NU), BF16),
            pltpu.VMEM((MD, ND), BF16),
            pltpu.VMEM((3, MD, Q), BF16),
            pltpu.VMEM((2, MD // 2, Q), BF16),
            pltpu.VMEM((2, TOK // 2, Q), BF16),
            pltpu.VMEM((2, 8, 256), F32),
            pltpu.VMEM((ITERS, 2, 1, MALL), F32),
            pltpu.VMEM((ITERS, 4, 1, MALL), F32),
            pltpu.VMEM((ITERS, 4, 1, NALL + 256), F32),
            pltpu.VMEM((ITERS, 4, 1, NALL + 256), F32),
            pltpu.VMEM((8, 1, 256), F32),
            pltpu.VMEM((4, 1, 256), F32),
            pltpu.VMEM((4, 1, 256), F32),
            pltpu.VMEM((8, 1, 256), F32),
            dma((6,)),
            dma((7,)),
            dma((7,)),
            dma((4, 4)),
            dma((4, 4)),
            dma((7, 4)),
            dma((7, 4)),
            dma((12, 8)),
            dma((12, 8)),
            dma((6,)),
            dma((6,)),
            dma((ITERS, 4, 3)),
            dma((ITERS, 4, 3)),
            dma((4, 7)),
            dma((4, 7)),
        ],
        compiler_params=pltpu.CompilerParams(
            collective_id=0, has_side_effects=True, vmem_limit_bytes=48 * 1024 * 1024
        ),
    )(weight_up, weight_down, inputs_up, grads_up, inputs_down, grads_down, vector_up, vector_down)
    return tuple(
        pl.pallas_call(
            scale,
            out_shape=(
                jax.ShapeDtypeStruct((MU, NU), BF16),
                jax.ShapeDtypeStruct((MD, ND), BF16),
                jax.ShapeDtypeStruct((2,), F32),
                jax.ShapeDtypeStruct((MU,), F32),
                jax.ShapeDtypeStruct((NU,), F32),
                jax.ShapeDtypeStruct((MD,), F32),
                jax.ShapeDtypeStruct((ND,), F32),
            ),
            in_specs=[smem] + [vmem] * 6,
            out_specs=(hbm, hbm, smem) + (vmem,) * 4,
            scratch_shapes=[
                pltpu.VMEM((MU, NU), BF16),
                pltpu.VMEM((MD, ND), BF16),
                dma((7,)),
            ],
            compiler_params=pltpu.CompilerParams(vmem_limit_bytes=24 * 1024 * 1024),
        )(gain_pair, *parts)
    )


def solution(mesh):
    in_specs = (
        P(), P("row", "col"), P("row", "col"), P("row", "col"), P("col", "row"),
        P("row", "col"), P("col", "row"), P("col"), P("col"),
    )
    out_specs = (P("row", "col"), P("row", "col"), P(), P("row"), P("col"), P("row"), P("col"))
    return jax.shard_map(local, mesh=mesh, in_specs=in_specs, out_specs=out_specs, check_vma=False)
```
